512 devices in a mesh: ctx: 16 (over y, core), head: 32 (over z, x).
Axes of the slice: x: 4, y: 8, z: 8, core: 2. Of those that a mesh axis runs over, the one named last changes fastest.
Arguments:
- query_rows: bfloat16 [6144, 64, 128], P('ctx', 'head'), may hold values from -1.75 to 1.75
- key_matrix: bfloat16 [6144, 64, 128], P('ctx', 'head'), may hold values from -1.75 to 1.75
- value_rows: bfloat16 [6144, 64, 128], P('ctx', 'head'), may hold values from -55 to 55
- decay_log: float32 [6144, 64], P('ctx', 'head'), may hold values from -0.6 to 0
- norm_gain: float32 [64, 128], P('head'), may hold values from 0.1 to 1.9
- grad_out: bfloat16 [6144, 64, 128], P('ctx', 'head'), may hold values from -6 to 6
Outputs:
- output: bfloat16 [6144, 64, 128], P('ctx', 'head')
- grad_query: bfloat16 [6144, 64, 128], P('ctx', 'head')
- grad_key: bfloat16 [6144, 64, 128], P('ctx', 'head')
- grad_value: bfloat16 [6144, 64, 128], P('ctx', 'head')
The draws below stay inside these ranges and needn't reach their ends.
All inputs are finite; a program needn't handle non-finite values.
Results may differ from the reference program's by a relative error of at most 0.019.
Values sent between devices are 32-bit elements; how exact they have to be, the bound alone decides.
A program may use at most 64 MiB of HBM per device.

```python
import math
import jax
import jax.numpy as jnp
from jax import lax

HEADS = 64
DK = 128
GROUP = 128
SEQUENCE_LENGTH = 6144


def draw_value_rows(key, part):
    key_base, key_scale = jax.random.split(key)
    spread = jax.random.uniform(key_scale, (HEADS, DK), jnp.float32)
    rising = jnp.arange(HEADS, dtype=jnp.float32) / max(HEADS - 1, 1)
    base = jnp.clip(jax.random.normal(key_base, (SEQUENCE_LENGTH, HEADS, DK), jnp.float32), -6.0, 6.0)
    scale = jnp.exp(spread * math.log(10.0) + rising[:, None] * math.log(3.0)) * 0.3
    return (base * scale[None]).astype(jnp.bfloat16)


def draw_decay_log(key, part):
    key_fast, key_quick, key_slow, key_rough, key_loss, key_spots = jax.random.split(key, 6)
    share = 0.5
    fast_heads = jax.random.uniform(key_fast, (HEADS,), jnp.float32) < share
    quick_rate = jnp.exp(jax.random.uniform(key_quick, (HEADS,), jnp.float32, math.log(1.0 / 50.0), math.log(1.0 / 30.0)))
    slow_rate = jnp.exp(jax.random.uniform(key_slow, (HEADS,), jnp.float32, math.log(0.05 / SEQUENCE_LENGTH), math.log(0.46 / SEQUENCE_LENGTH)))
    decay_rates = jnp.where(fast_heads, quick_rate, slow_rate)
    coarse_values = jax.random.uniform(key_rough, (SEQUENCE_LENGTH, HEADS), jnp.float32, 0.5, 1.5)
    sample_points = jax.random.randint(key_spots, (3,), 0, SEQUENCE_LENGTH)
    sudden_decay = jnp.any(jnp.arange(SEQUENCE_LENGTH)[:, None] == sample_points[None, :], axis=1)
    loss_values = jax.random.uniform(key_loss, (SEQUENCE_LENGTH, HEADS), jnp.float32, 0.2, 0.4)
    return -decay_rates[None, :] * coarse_values + jnp.where(sudden_decay[:, None], jnp.log1p(-loss_values), 0.0)


def block_levels(key, extent, cuts, least, high):
    def one(dim, shards_of):
        draws = jax.random.uniform(jax.random.fold_in(jax.random.fold_in(key, 6), dim), (shards_of,), jnp.float32, least / len(cuts), high / len(cuts))
        return jnp.repeat(jnp.exp(draws), extent[dim] // shards_of).reshape((-1,) + (1,) * (len(extent) - dim - 1))

    gain = one(*cuts[0])
    for cut in cuts[1:]:
        gain = gain * one(*cut)
    return gain


def normal_values(key, shape, scale, bound, cuts=(), kind=jnp.bfloat16):
    loudness = block_levels(key, shape, cuts, -0.22, 0.18) if cuts else 1.0
    drawn = jax.random.normal(key, shape, jnp.float32) * scale * loudness
    return jnp.minimum(jnp.maximum(drawn, -bound), bound).astype(kind)


def setup_inputs(seed: int = 0) -> dict:
    streams_of = jax.random.split(jax.random.key(seed), 7)
    return {
        "query_rows": normal_values(streams_of[0], (SEQUENCE_LENGTH, HEADS, DK), 0.3, 1.75, ((0, 16), (1, 32))),
        "key_matrix": normal_values(streams_of[1], (SEQUENCE_LENGTH, HEADS, DK), 0.3, 1.75, ((0, 16), (1, 32))),
        "value_rows": draw_value_rows(jax.random.fold_in(streams_of[6], 71), 0),
        "decay_log": draw_decay_log(jax.random.fold_in(streams_of[6], 71), 0),
        "norm_gain": jnp.clip(1.0 + 0.18 * jax.random.normal(streams_of[4], (HEADS, DK), jnp.float32), 0.1, 1.9),
        "grad_out": normal_values(streams_of[5], (SEQUENCE_LENGTH, HEADS, DK), 1.0, 6.0, ((0, 16), (1, 32))),
    }


epsilon = 1e-06

def decays(log_rates):
    cumulative = jnp.cumsum(log_rates, axis=1)
    block_total = cumulative[:, -1]
    row_ids = lax.broadcasted_iota(jnp.int32, (GROUP, GROUP), 0)
    col_ids = lax.broadcasted_iota(jnp.int32, (GROUP, GROUP), 1)
    causal = (row_ids >= col_ids)[None]
    spread = cumulative[:, :, None] - cumulative[:, None, :]
    mask_weight = jnp.where(causal, jnp.exp(jnp.where(causal, spread, 0.0)), 0.0)
    return (cumulative, block_total, mask_weight)

def forward_states(key_matrix, value_rows, cumulative, block_total):

    def advance(carry_state, pieces):
        key_part, value_part, cum_part, total_part = pieces
        decayed = (key_part * jnp.exp(total_part - cum_part)[:, None]).astype(jnp.bfloat16)
        fresh_term = jnp.dot(decayed.T, value_part, preferred_element_type=jnp.float32)
        return (jnp.exp(total_part) * carry_state + fresh_term, carry_state)
    start = jnp.zeros((key_matrix.shape[2], value_rows.shape[2]), jnp.float32)
    return lax.scan(advance, start, (key_matrix, value_rows, cumulative, block_total))[1].astype(jnp.bfloat16)

def backward_states(query_rows, grad_rows, cumulative, block_total):

    def retreat(carry_state, pieces):
        query_part, grad_part, cum_part, total_part = pieces
        decayed = (query_part * jnp.exp(cum_part)[:, None]).astype(jnp.bfloat16)
        fresh_term = jnp.dot(decayed.T, grad_part, preferred_element_type=jnp.float32)
        return (jnp.exp(total_part) * carry_state + fresh_term, carry_state)
    start = jnp.zeros((query_rows.shape[2], grad_rows.shape[2]), jnp.float32)
    return lax.scan(retreat, start, (query_rows, grad_rows, cumulative, block_total), reverse=True)[1].astype(jnp.bfloat16)

def local_weights(query_rows, key_matrix, mask_weight):
    scores = jnp.einsum('cid,cjd->cij', query_rows.astype(jnp.float32), key_matrix.astype(jnp.float32))
    return (scores * mask_weight).astype(jnp.bfloat16)

def head_forward(pieces):
    query_rows, key_matrix, value_rows, log_rates = pieces
    cumulative, block_total, mask_weight = decays(log_rates)
    attn_weights = local_weights(query_rows, key_matrix, mask_weight)
    local_part = jnp.einsum('cij,cjd->cid', attn_weights.astype(jnp.float32), value_rows.astype(jnp.float32))
    state_bf = forward_states(key_matrix, value_rows, cumulative, block_total)
    carried_part = jnp.einsum('cid,cde->cie', query_rows.astype(jnp.float32), state_bf.astype(jnp.float32)) * jnp.exp(cumulative)[:, :, None]
    return (local_part + carried_part).astype(jnp.bfloat16)

def head_backward(pieces):
    query_rows, key_matrix, value_rows, log_rates, grad_rows = pieces
    cumulative, block_total, mask_weight = decays(log_rates)
    attn_weights = local_weights(query_rows, key_matrix, mask_weight)
    query_f = query_rows.astype(jnp.float32)
    key_f = key_matrix.astype(jnp.float32)
    value_f = value_rows.astype(jnp.float32)
    grad_f = grad_rows.astype(jnp.float32)
    grad_dots = jnp.einsum('cie,cje->cij', grad_f, value_f)
    grad_scores = (grad_dots * mask_weight).astype(jnp.bfloat16).astype(jnp.float32)
    query_local = jnp.einsum('cij,cjd->cid', grad_scores, key_f)
    key_local = jnp.einsum('cij,cid->cjd', grad_scores, query_f)
    value_local = jnp.einsum('cij,cie->cje', attn_weights.astype(jnp.float32), grad_f)
    state_bf = forward_states(key_matrix, value_rows, cumulative, block_total).astype(jnp.float32)
    query_carried = jnp.einsum('cie,cde->cid', grad_f, state_bf) * jnp.exp(cumulative)[:, :, None]
    back_bf = backward_states(query_rows, grad_rows, cumulative, block_total).astype(jnp.float32)
    tail = jnp.exp(block_total[:, None] - cumulative)[:, :, None]
    key_carried = jnp.einsum('cie,cde->cid', value_f, back_bf) * tail
    value_carried = jnp.einsum('cid,cde->cie', key_f, back_bf) * tail
    return ((query_local + query_carried).astype(jnp.bfloat16), (key_local + key_carried).astype(jnp.bfloat16), (value_local + value_carried).astype(jnp.bfloat16))

def reference(query_rows, key_matrix, value_rows, decay_log, norm_gain, grad_out):
    seq_len, head_count, head_size = query_rows.shape
    num_blocks = seq_len // GROUP

    def by_head(array):
        return jnp.moveaxis(array, 1, 0).reshape(head_count, num_blocks, GROUP, head_size)

    def by_position(array):
        return jnp.moveaxis(array.reshape(head_count, seq_len, head_size), 0, 1)
    query_heads = by_head(query_rows)
    key_heads = by_head(key_matrix)
    value_heads = by_head(value_rows)
    log_heads = decay_log.T.reshape(head_count, num_blocks, GROUP)
    attention = by_position(lax.map(head_forward, (query_heads, key_heads, value_heads, log_heads)))
    attn_f = attention.astype(jnp.float32)
    features = head_count * head_size
    inv_rms = lax.rsqrt(lax.optimization_barrier(jnp.sum(attn_f * attn_f, axis=(1, 2))) / features + epsilon)
    output = (attn_f * inv_rms[:, None, None] * norm_gain[None]).astype(jnp.bfloat16)
    full_grad = grad_out.astype(jnp.float32) + output.astype(jnp.float32)
    scaled_grad = norm_gain[None] * full_grad
    inner = lax.optimization_barrier(jnp.sum(scaled_grad * attn_f, axis=(1, 2)))
    grad_attention = (inv_rms[:, None, None] * scaled_grad - attn_f * (inv_rms ** 3 * inner / features)[:, None, None]).astype(jnp.bfloat16)
    gradient_per_head = by_head(grad_attention)
    grad_q, grad_k, grad_v = lax.map(head_backward, (query_heads, key_heads, value_heads, log_heads, gradient_per_head))
    return (output, by_position(grad_q), by_position(grad_k), by_position(grad_v))
```

```python
import functools

import jax
import jax.numpy as jnp
from jax import lax
from jax.experimental import pallas as pl
from jax.experimental.pallas import tpu as pltpu
from jax.sharding import PartitionSpec as P

GROUP = 128
EPSILON = 1e-06
F32 = jnp.float32
BF16 = jnp.bfloat16
MESH = pl.DeviceIdType.MESH


def dot(a, b, over):
    return lax.dot_general(a, b, (over, ((), ())), preferred_element_type=F32)


def nn(a, b):
    return dot(a, b, ((1,), (0,)))


def nt(a, b):
    return dot(a, b, ((1,), (1,)))


def tn(a, b):
    return dot(a, b, ((0,), (0,)))


def kernel(
    sizes,
    q_hbm, k_hbm, v_hbm, g_hbm, decay, gain,
    out_hbm, gq_hbm, gk_hbm, gv_hbm,
    q, k, v, g, out, gq, gk, gv,
    mask, weights, dots, attn, grad, part, value_part, key_part,
    rise, tail, fresh, states, backs, wide_k, wide_q,
    factor, ends, seen, made, came, ends2, seen2, made2, came2,
    sums, sums_x, sums2, sums_z,
    in_sem, out_sem, send_sem, recv_sem,
):
    ranks, inner_size, outer_size, blocks, features = sizes
    rows = 2 * GROUP
    pos = lax.axis_index("ctx")
    head = lax.axis_index("head")
    outer, inner = head // inner_size, head % inner_size

    order = sorted(range(1, ranks), key=lambda s: -min(s, ranks - s))
    ctx_peers = {s: lax.rem(pos + s, ranks) for s in order}
    x_peers = {s: outer * inner_size + lax.rem(inner + s, inner_size) for s in range(1, inner_size)}
    z_peers = {s: lax.rem(outer + s, outer_size) * inner_size + inner for s in range(1, outer_size)}

    barrier = pltpu.get_barrier_semaphore()
    for s in order:
        pl.semaphore_signal(barrier, 1, device_id={"ctx": ctx_peers[s]}, device_id_type=MESH)
    for peer in list(x_peers.values()) + list(z_peers.values()):
        pl.semaphore_signal(barrier, 1, device_id={"head": peer}, device_id_type=MESH)

    loads = []
    for i, (src, dst) in enumerate(((k_hbm, k), (v_hbm, v), (q_hbm, q), (g_hbm, g))):
        loads.append(pltpu.make_async_copy(src, dst, in_sem.at[i]))
        loads[-1].start()

    def send(stage, s, src, dst, where):
        copy = pltpu.make_async_remote_copy(
            src_ref=src, dst_ref=dst,
            send_sem=send_sem.at[stage, s], recv_sem=recv_sem.at[stage, s],
            device_id=where, device_id_type=MESH,
        )
        copy.start()
        return copy

    row = lax.broadcasted_iota(jnp.int32, (rows, 128), 0)
    lane = lax.broadcasted_iota(jnp.int32, (rows, 128), 1)
    even = (row % 2) == 0
    token = row // 2
    big_row = lax.broadcasted_iota(jnp.int32, (rows, rows), 0)
    big_col = lax.broadcasted_iota(jnp.int32, (rows, rows), 1)

    def block(c):
        return pl.ds(c * rows, rows)

    def wide(x):
        return jnp.concatenate(
            [jnp.where(even, x, 0.0).astype(BF16), jnp.where(even, 0.0, x).astype(BF16)], axis=1
        )

    def own_head(x):
        return jnp.where(even, x[:, :128], x[:, 128:])

    block_decay = []
    total = jnp.zeros((2, 1), F32)
    cums = []
    for c in range(blocks):
        a = decay[:, c * GROUP:(c + 1) * GROUP]
        spread = jnp.where(even, a[0:1, :], a[1:2, :])
        cum = jnp.sum(jnp.where(lane <= token, spread, 0.0), axis=1, keepdims=True)
        end = jnp.sum(a, axis=1, keepdims=True)
        total = total + end
        end_rows = jnp.where(even, end[0:1, :], end[1:2, :])
        cum_full = jnp.broadcast_to(cum, (rows, 128))
        rise[c] = jnp.exp(cum_full)
        tail[c] = jnp.exp(end_rows - cum_full)
        block_decay.append(
            jnp.exp(jnp.where(row < 128, end[0:1, :], end[1:2, :]))
        )
        cums.append(cum)
    factor[pos] = jnp.broadcast_to(jnp.exp(total), (2, 128))

    loads[0].wait()
    loads[1].wait()
    state = jnp.zeros((rows, 128), F32)
    for c in range(blocks):
        decayed = k[block(c), :].astype(F32) * tail[c]
        term = tn(wide(decayed), v[block(c), :])
        fresh[c] = term
        state = term if c == 0 else block_decay[c] * state + term
    per = rows // ranks
    ends[...] = state.reshape(ranks, per, 128)

    pl.semaphore_wait(barrier, (ranks - 1) + (inner_size - 1) + (outer_size - 1))
    copies = []

    factor_copies = [
        send(0, s, factor.at[pos], factor.at[pos], {"ctx": ctx_peers[s]}) for s in order
    ]
    copies += factor_copies

    def scatter(stage, src, dst):
        sent = [send(stage, s, src.at[ctx_peers[s]], dst.at[pos], {"ctx": ctx_peers[s]}) for s in order]
        copies.extend(sent)
        dst[pos] = src[pos]
        return sent

    def arrive(sent):
        for copy in sent:
            copy.wait_recv()

    first = scatter(1, ends, seen)

    loads[2].wait()
    loads[3].wait()
    same = (big_row % 2 == big_col % 2) & (big_row >= big_col)

    def local_forward(c):
        cum = jnp.broadcast_to(cums[c], (rows, rows))
        across = jnp.sum(jnp.where(big_row == big_col, cum, 0.0), axis=0, keepdims=True)
        m = jnp.where(same, jnp.exp(jnp.where(same, cum - across, 0.0)), 0.0)
        mask[c] = m
        w = (nt(q[block(c), :], k[block(c), :]) * m).astype(BF16)
        weights[c] = w
        part[c] = nn(w, v[block(c), :])

    half = (blocks + 1) // 2
    for c in range(half):
        local_forward(c)

    arrive(factor_copies)
    arrive(first)
    mine = pos * per < 128

    def rank_factor(n):
        f = factor[n]
        return jnp.where(mine, f[0:1, :], f[1:2, :])

    carry = jnp.zeros((per, 128), F32)
    for n in range(ranks):
        made[n] = carry
        if n + 1 < ranks:
            carry = rank_factor(n) * carry + seen[n]
    second = scatter(2, made, came)

    for c in range(half, blocks):
        local_forward(c)
    for c in range(blocks):
        wide_k[c] = wide(k[block(c), :].astype(F32))

    arrive(second)
    state = came[...].reshape(rows, 128)
    for c in range(blocks):
        if c:
            state = block_decay[c - 1] * state + fresh[c - 1]
        states[c] = state.astype(BF16)

    gain_rows = jnp.where(even, gain[0:1, :], gain[1:2, :])
    pick = token == lane

    def per_token(x):
        col = jnp.sum(x, axis=1, keepdims=True)
        return jnp.sum(jnp.where(pick, col, 0.0), axis=0, keepdims=True)

    sums[...] = jnp.zeros_like(sums)
    for c in range(blocks):
        carried = nn(wide(q[block(c), :].astype(F32)), states[c])
        a_bf = (part[c] + carried * rise[c]).astype(BF16)
        attn[c] = a_bf
        a = a_bf.astype(F32)
        ga = gain_rows * a
        sums[3 * c:3 * c + 1, :] = per_token(a * a)
        sums[3 * c + 1:3 * c + 2, :] = per_token(ga * g[block(c), :].astype(F32))
        sums[3 * c + 2:3 * c + 3, :] = per_token(ga * ga)

    x_sent = [send(3, s, sums, sums_x.at[s - 1], {"head": x_peers[s]}) for s in x_peers]
    copies += x_sent
    for c in range(blocks):
        wide_q[c] = wide(q[block(c), :].astype(F32) * rise[c])
    arrive(x_sent)
    acc = sums[...]
    for s in x_peers:
        acc = acc + sums_x[s - 1]
    sums2[...] = acc
    z_sent = [send(4, s, sums2, sums_z.at[s - 1], {"head": z_peers[s]}) for s in z_peers]
    copies += z_sent
    arrive(z_sent)
    for s in z_peers:
        acc = acc + sums_z[s - 1]

    def to_rows(x):
        return jnp.sum(jnp.where(pick, x, 0.0), axis=1, keepdims=True)

    stores = []

    def store(i, src, dst):
        copy = pltpu.make_async_copy(src, dst, out_sem.at[i])
        copy.start()
        stores.append(copy)

    for c in range(blocks):
        inv = lax.rsqrt(acc[3 * c:3 * c + 1, :] / features + EPSILON)
        total_inner = acc[3 * c + 1:3 * c + 2, :] + inv * acc[3 * c + 2:3 * c + 3, :]
        shrink = inv * inv * inv * total_inner / features
        inv_col = to_rows(inv)
        shrink_col = to_rows(shrink)
        a = attn[c].astype(F32)
        o = (a * inv_col * gain_rows).astype(BF16)
        out[block(c), :] = o
        scaled = gain_rows * (g[block(c), :].astype(F32) + o.astype(F32))
        grad[c] = (inv_col * scaled - a * shrink_col).astype(BF16)

    for c in reversed(range(blocks)):
        term = tn(wide_q[c], grad[c])
        fresh[c] = term
        state = term if c == blocks - 1 else block_decay[c] * state + term
    ends2[...] = state.reshape(ranks, per, 128)
    third = scatter(5, ends2, seen2)
    store(0, out, out_hbm)

    def local_dots(c):
        d = (nt(grad[c], v[block(c), :]) * mask[c]).astype(BF16)
        dots[c] = d
        carried = own_head(nt(grad[c], states[c]))
        gq[block(c), :] = (nn(d, k[block(c), :]) + carried * rise[c]).astype(BF16)

    def local_backward(c):
        key_part[c] = tn(dots[c], q[block(c), :])
        value_part[c] = tn(weights[c], grad[c])

    for c in range(blocks):
        local_dots(c)
    store(1, gq, gq_hbm)

    arrive(third)
    carry = jnp.zeros((per, 128), F32)
    for n in reversed(range(ranks)):
        made2[n] = carry
        if n:
            carry = rank_factor(n) * carry + seen2[n]
    fourth = scatter(6, made2, came2)
    for c in range(blocks):
        local_backward(c)

    arrive(fourth)
    state = came2[...].reshape(rows, 128)
    for c in reversed(range(blocks)):
        if c < blocks - 1:
            state = block_decay[c + 1] * state + fresh[c + 1]
        backs[c] = state.astype(BF16)
    for c in range(blocks):
        key_carried = own_head(nt(v[block(c), :], backs[c]))
        gk[block(c), :] = (key_part[c] + key_carried * tail[c]).astype(BF16)
        value_carried = nn(wide_k[c], backs[c])
        gv[block(c), :] = (value_part[c] + value_carried * tail[c]).astype(BF16)
    store(2, gk, gk_hbm)
    store(3, gv, gv_hbm)
    for copy in copies:
        copy.wait_send()
    for copy in stores:
        copy.wait()


def per_device(ranks, head_ranks, inner_size, query_rows, key_matrix, value_rows, decay_log, norm_gain, grad_out):
    tokens, heads, size = query_rows.shape
    blocks = tokens // GROUP
    rows = 2 * GROUP
    per = rows // ranks
    outer_size = head_ranks // inner_size
    flat = (tokens * heads, size)
    sizes = (ranks, inner_size, outer_size, blocks, heads * head_ranks * size)
    vm = pltpu.VMEM
    sum_rows = -(-3 * blocks // 8) * 8
    any_spec = pl.BlockSpec(memory_space=pl.ANY)
    vmem_spec = pl.BlockSpec(memory_space=pltpu.VMEM)
    state_slots = [vm((ranks, per, 128), F32)] * 4
    results = pl.pallas_call(
        functools.partial(kernel, sizes),
        out_shape=[jax.ShapeDtypeStruct(flat, BF16)] * 4,
        in_specs=[any_spec] * 4 + [vmem_spec] * 2,
        out_specs=[any_spec] * 4,
        scratch_shapes=[vm(flat, BF16)] * 8
        + [
            vm((blocks, rows, rows), F32),
            vm((blocks, rows, rows), BF16),
            vm((blocks, rows, rows), BF16),
            vm((blocks, rows, 128), BF16),
            vm((blocks, rows, 128), BF16),
            vm((blocks, rows, 128), F32),
            vm((blocks, rows, 128), F32),
            vm((blocks, rows, 128), F32),
            vm((blocks, rows, 128), F32),
            vm((blocks, rows, 128), F32),
            vm((blocks, rows, 128), F32),
            vm((blocks, rows, 128), BF16),
            vm((blocks, rows, 128), BF16),
            vm((blocks, rows, rows), BF16),
            vm((blocks, rows, rows), BF16),
            vm((ranks, 2, 128), F32),
        ]
        + state_slots
        + state_slots
        + [
            vm((sum_rows, 128), F32),
            vm((inner_size - 1, sum_rows, 128), F32),
            vm((sum_rows, 128), F32),
            vm((outer_size - 1, sum_rows, 128), F32),
            pltpu.SemaphoreType.DMA((4,)),
            pltpu.SemaphoreType.DMA((4,)),
            pltpu.SemaphoreType.DMA((7, ranks)),
            pltpu.SemaphoreType.DMA((7, ranks)),
        ],
        compiler_params=pltpu.CompilerParams(collective_id=0, has_side_effects=True),
        name="lightning",
    )(
        query_rows.reshape(flat),
        key_matrix.reshape(flat),
        value_rows.reshape(flat),
        grad_out.reshape(flat),
        decay_log.T,
        norm_gain,
    )
    return tuple(r.reshape(tokens, heads, size) for r in results)


def solution(mesh):
    ranks, head_ranks = mesh.shape["ctx"], mesh.shape["head"]
    inner_size = 4 if head_ranks % 4 == 0 and head_ranks > 4 else 1
    rows = P("ctx", "head", None)
    return jax.shard_map(
        functools.partial(per_device, ranks, head_ranks, inner_size),
        mesh=mesh,
        in_specs=(rows, rows, rows, P("ctx", "head"), P("head", None), rows),
        out_specs=(rows,) * 4,
        check_vma=False,
    )
```

```python
import functools

import jax
import jax.numpy as jnp
from jax import lax
from jax.experimental import pallas as pl
from jax.experimental.pallas import tpu as pltpu
from jax.sharding import PartitionSpec as P

GROUP = 128
EPSILON = 1e-06
F32 = jnp.float32
BF16 = jnp.bfloat16
MESH = pl.DeviceIdType.MESH


def dot(a, b, over):
    return lax.dot_general(a, b, (over, ((), ())), preferred_element_type=F32)


def nn(a, b):
    return dot(a, b, ((1,), (0,)))


def nt(a, b):
    return dot(a, b, ((1,), (1,)))


def tn(a, b):
    return dot(a, b, ((0,), (0,)))


def kernel(
    sizes,
    q_hbm, k_hbm, v_hbm, g_hbm, decay_hbm, gain_hbm,
    out, gq, gk, gv,
    q, k, v, g, decay, gain,
    mask, weights, dots, attn, grad, part, value_part, key_part,
    rise, tail, fresh, states, backs, wide_k, wide_q, plain_q,
    factor, ends, seen, made, came, ends2, seen2, made2, came2,
    sums, sums_x, sums2, sums_z,
    in_sem, send_sem, recv_sem,
):
    ranks, inner_size, outer_size, blocks, features = sizes
    rows = 2 * GROUP
    pos = lax.axis_index("ctx")
    head = lax.axis_index("head")
    outer, inner = head // inner_size, head % inner_size

    order = sorted(range(1, ranks), key=lambda s: -min(s, ranks - s))
    ctx_peers = {s: lax.rem(pos + s, ranks) for s in order}
    x_peers = {s: outer * inner_size + lax.rem(inner + s, inner_size) for s in range(1, inner_size)}
    z_peers = {s: lax.rem(outer + s, outer_size) * inner_size + inner for s in range(1, outer_size)}

    loads = []
    pairs = (k_hbm, k), (v_hbm, v), (q_hbm, q), (g_hbm, g), (gain_hbm, gain), (decay_hbm, decay)
    for i, (src, dst) in reversed(list(enumerate(pairs))):
        loads.insert(0, pltpu.make_async_copy(src, dst, in_sem.at[i]))
        loads[0].start()

    barrier = pltpu.get_barrier_semaphore()
    for s in order:
        pl.semaphore_signal(barrier, 1, device_id={"ctx": ctx_peers[s]}, device_id_type=MESH)
    for peer in list(x_peers.values()) + list(z_peers.values()):
        pl.semaphore_signal(barrier, 1, device_id={"head": peer}, device_id_type=MESH)

    def send(stage, s, src, dst, where):
        copy = pltpu.make_async_remote_copy(
            src_ref=src, dst_ref=dst,
            send_sem=send_sem.at[stage, s], recv_sem=recv_sem.at[stage, s],
            device_id=where, device_id_type=MESH,
        )
        copy.start()
        return copy

    row = lax.broadcasted_iota(jnp.int32, (rows, 128), 0)
    lane = lax.broadcasted_iota(jnp.int32, (rows, 128), 1)
    even = (row % 2) == 0
    token = row // 2
    big_row = lax.broadcasted_iota(jnp.int32, (rows, rows), 0)
    big_col = lax.broadcasted_iota(jnp.int32, (rows, rows), 1)

    def block(c):
        return pl.ds(c * rows, rows)

    def wide(x):
        return jnp.concatenate(
            [jnp.where(even, x, 0.0).astype(BF16), jnp.where(even, 0.0, x).astype(BF16)], axis=1
        )

    def own_head(x):
        return jnp.where(even, x[:, :128], x[:, 128:])

    loads[5].wait()
    block_decay = []
    total = jnp.zeros((2, 1), F32)
    cums = []
    for c in range(blocks):
        a = decay[:, c * GROUP:(c + 1) * GROUP]
        spread = jnp.where(even, a[0:1, :], a[1:2, :])
        cum = jnp.sum(jnp.where(lane <= token, spread, 0.0), axis=1, keepdims=True)
        end = jnp.sum(a, axis=1, keepdims=True)
        total = total + end
        end_rows = jnp.where(even, end[0:1, :], end[1:2, :])
        cum_full = jnp.broadcast_to(cum, (rows, 128))
        rise[c] = jnp.exp(cum_full)
        tail[c] = jnp.exp(end_rows - cum_full)
        block_decay.append(
            jnp.exp(jnp.where(row < 128, end[0:1, :], end[1:2, :]))
        )
        cums.append(cum)
    factor[pos] = jnp.broadcast_to(jnp.exp(total), (2, 128))

    loads[0].wait()
    loads[1].wait()
    state = jnp.zeros((rows, 128), F32)
    for c in range(blocks):
        decayed = k[block(c), :].astype(F32) * tail[c]
        term = tn(wide(decayed), v[block(c), :])
        fresh[c] = term
        state = term if c == 0 else block_decay[c] * state + term
    per = rows // ranks
    ends[...] = state.reshape(ranks, 2, per // 2, 128)

    pl.semaphore_wait(barrier, (ranks - 1) + (inner_size - 1) + (outer_size - 1))
    copies = []

    factor_copies = [
        send(0, s, factor.at[pos], factor.at[pos], {"ctx": ctx_peers[s]}) for s in order
    ]
    copies += factor_copies

    def scatter(stage, half, src, dst):
        sent = [
            send(stage + half, s, src.at[ctx_peers[s], half], dst.at[pos, half], {"ctx": ctx_peers[s]})
            for s in order
        ]
        copies.extend(sent)
        dst[pos, half] = src[pos, half]
        return sent

    def arrive(sent):
        for copy in sent:
            copy.wait_recv()

    first = [scatter(3, half, ends, seen) for half in range(2)]

    loads[2].wait()
    loads[3].wait()
    same = (big_row % 2 == big_col % 2) & (big_row >= big_col)

    def local_forward(c):
        cum = jnp.broadcast_to(cums[c], (rows, rows))
        across = jnp.sum(jnp.where(big_row == big_col, cum, 0.0), axis=0, keepdims=True)
        m = jnp.where(same, jnp.exp(jnp.where(same, cum - across, 0.0)), 0.0)
        mask[c] = m
        w = (nt(q[block(c), :], k[block(c), :]) * m).astype(BF16)
        weights[c] = w
        part[c] = nn(w, v[block(c), :])

    for c in range(blocks):
        local_forward(c)

    arrive(factor_copies)
    mine = pos * per < 128

    def rank_factor(n):
        f = factor[n]
        return jnp.where(mine, f[0:1, :], f[1:2, :])

    def scan_ranks(steps, src, dst, half):
        carry = jnp.zeros((per // 2, 128), F32)
        for n in steps:
            dst[n, half] = carry
            if n != steps[-1]:
                carry = rank_factor(n) * carry + src[n, half]

    second = []
    for half in range(2):
        arrive(first[half])
        scan_ranks(list(range(ranks)), seen, made, half)
        second.append(scatter(5, half, made, came))

    for c in range(blocks):
        q_block = q[block(c), :].astype(F32)
        wide_k[c] = wide(k[block(c), :].astype(F32))
        wide_q[c] = wide(q_block * rise[c])
        plain_q[c] = wide(q_block)

    loads[4].wait()
    arrive(second[0])
    arrive(second[1])
    state = came[...].reshape(rows, 128)
    for c in range(blocks):
        if c:
            state = block_decay[c - 1] * state + fresh[c - 1]
        states[c] = state.astype(BF16)

    gain_rows = jnp.where(even, gain[0:1, :], gain[1:2, :])
    pick = token == lane

    def per_token(x):
        col = jnp.sum(x, axis=1, keepdims=True)
        return jnp.sum(jnp.where(pick, col, 0.0), axis=0, keepdims=True)

    for c in range(blocks):
        carried = nn(plain_q[c], states[c])
        a_bf = (part[c] + carried * rise[c]).astype(BF16)
        attn[c] = a_bf
        a = a_bf.astype(F32)
        ga = gain_rows * a
        sums[3 * c:3 * c + 1, :] = per_token(a * a)
        sums[3 * c + 1:3 * c + 2, :] = per_token(ga * g[block(c), :].astype(F32))
        sums[3 * c + 2:3 * c + 3, :] = per_token(ga * ga)

    x_sent = [send(1, s, sums, sums_x.at[s - 1], {"head": x_peers[s]}) for s in x_peers]
    copies += x_sent
    arrive(x_sent)
    acc = sums[...]
    for s in x_peers:
        acc = acc + sums_x[s - 1]
    sums2[...] = acc
    z_sent = [send(2, s, sums2, sums_z.at[s - 1], {"head": z_peers[s]}) for s in z_peers]
    copies += z_sent
    arrive(z_sent)
    for s in z_peers:
        acc = acc + sums_z[s - 1]

    def to_rows(x):
        return jnp.sum(jnp.where(pick, x, 0.0), axis=1, keepdims=True)

    for c in range(blocks):
        inv = lax.rsqrt(acc[3 * c:3 * c + 1, :] / features + EPSILON)
        total_inner = acc[3 * c + 1:3 * c + 2, :] + inv * acc[3 * c + 2:3 * c + 3, :]
        shrink = inv * inv * inv * total_inner / features
        inv_col = to_rows(inv)
        shrink_col = to_rows(shrink)
        a = attn[c].astype(F32)
        o = (a * inv_col * gain_rows).astype(BF16)
        out[block(c), :] = o
        scaled = gain_rows * (g[block(c), :].astype(F32) + o.astype(F32))
        grad[c] = (inv_col * scaled - a * shrink_col).astype(BF16)

    for c in reversed(range(blocks)):
        term = tn(wide_q[c], grad[c])
        fresh[c] = term
        state = term if c == blocks - 1 else block_decay[c] * state + term
    ends2[...] = state.reshape(ranks, 2, per // 2, 128)
    third = [scatter(7, half, ends2, seen2) for half in range(2)]

    def local_dots(c):
        d = (nt(grad[c], v[block(c), :]) * mask[c]).astype(BF16)
        dots[c] = d
        carried = own_head(nt(grad[c], states[c]))
        gq[block(c), :] = (nn(d, k[block(c), :]) + carried * rise[c]).astype(BF16)

    def local_backward(c):
        key_part[c] = tn(dots[c], q[block(c), :])
        value_part[c] = tn(weights[c], grad[c])

    for c in range(blocks):
        local_dots(c)
    for c in range(blocks):
        local_backward(c)

    fourth = []
    for half in range(2):
        arrive(third[half])
        scan_ranks(list(reversed(range(ranks))), seen2, made2, half)
        fourth.append(scatter(9, half, made2, came2))

    arrive(fourth[0])
    arrive(fourth[1])
    state = came2[...].reshape(rows, 128)
    for c in reversed(range(blocks)):
        if c < blocks - 1:
            state = block_decay[c + 1] * state + fresh[c + 1]
        backs[c] = state.astype(BF16)
    for c in range(blocks):
        key_carried = own_head(nt(v[block(c), :], backs[c]))
        gk[block(c), :] = (key_part[c] + key_carried * tail[c]).astype(BF16)
        value_carried = nn(wide_k[c], backs[c])
        gv[block(c), :] = (value_part[c] + value_carried * tail[c]).astype(BF16)
    for copy in copies:
        copy.wait_send()


def write_out(a, b, c, d, oa, ob, oc, od, sem):
    copies = [
        pltpu.make_async_copy(src, dst, sem.at[i])
        for i, (src, dst) in enumerate(((a, oa), (b, ob), (c, oc), (d, od)))
    ]
    for copy in copies:
        copy.start()
    for copy in copies:
        copy.wait()


def per_device(ranks, head_ranks, inner_size, query_rows, key_matrix, value_rows, decay_log, norm_gain, grad_out):
    tokens, heads, size = query_rows.shape
    blocks = tokens // GROUP
    rows = 2 * GROUP
    per = rows // ranks
    outer_size = head_ranks // inner_size
    flat = (tokens * heads, size)
    sizes = (ranks, inner_size, outer_size, blocks, heads * head_ranks * size)
    vm = pltpu.VMEM
    sum_rows = 3 * blocks
    any_spec = pl.BlockSpec(memory_space=pl.ANY)
    vmem_spec = pl.BlockSpec(memory_space=pltpu.VMEM)
    state_slots = [vm((ranks, 2, per // 2, 128), F32)] * 4
    results = pl.pallas_call(
        functools.partial(kernel, sizes),
        out_shape=[pltpu.VMEM(flat, BF16)] * 4,
        in_specs=[any_spec] * 6,
        out_specs=[vmem_spec] * 4,
        scratch_shapes=[vm(flat, BF16)] * 4
        + [
            vm(decay_log.T.shape, F32),
            vm(norm_gain.shape, F32),
            vm((blocks, rows, rows), F32),
            vm((blocks, rows, rows), BF16),
            vm((blocks, rows, rows), BF16),
            vm((blocks, rows, 128), BF16),
            vm((blocks, rows, 128), BF16),
            vm((blocks, rows, 128), F32),
            vm((blocks, rows, 128), F32),
            vm((blocks, rows, 128), F32),
            vm((blocks, rows, 128), F32),
            vm((blocks, rows, 128), F32),
            vm((blocks, rows, 128), F32),
            vm((blocks, rows, 128), BF16),
            vm((blocks, rows, 128), BF16),
            vm((blocks, rows, rows), BF16),
            vm((blocks, rows, rows), BF16),
            vm((blocks, rows, rows), BF16),
            vm((ranks, 2, 128), F32),
        ]
        + state_slots
        + state_slots
        + [
            vm((sum_rows, 128), F32),
            vm((inner_size - 1, sum_rows, 128), F32),
            vm((sum_rows, 128), F32),
            vm((outer_size - 1, sum_rows, 128), F32),
            pltpu.SemaphoreType.DMA((6,)),
            pltpu.SemaphoreType.DMA((11, ranks)),
            pltpu.SemaphoreType.DMA((11, ranks)),
        ],
        compiler_params=pltpu.CompilerParams(collective_id=0, has_side_effects=True),
        name="lightning",
    )(
        query_rows.reshape(flat),
        key_matrix.reshape(flat),
        value_rows.reshape(flat),
        grad_out.reshape(flat),
        decay_log.T,
        norm_gain,
    )
    results = pl.pallas_call(
        write_out,
        out_shape=[jax.ShapeDtypeStruct(flat, BF16)] * 4,
        in_specs=[vmem_spec] * 4,
        out_specs=[any_spec] * 4,
        scratch_shapes=[pltpu.SemaphoreType.DMA((4,))],
        name="write_out",
    )(*[pltpu.with_memory_space_constraint(r, pltpu.VMEM) for r in results])
    return tuple(r.reshape(tokens, heads, size) for r in results)


def solution(mesh):
    ranks, head_ranks = mesh.shape["ctx"], mesh.shape["head"]
    inner_size = 4 if head_ranks % 4 == 0 and head_ranks > 4 else 1
    rows = P("ctx", "head", None)
    return jax.shard_map(
        functools.partial(per_device, ranks, head_ranks, inner_size),
        mesh=mesh,
        in_specs=(rows, rows, rows, P("ctx", "head"), P("head", None), rows),
        out_specs=(rows,) * 4,
        check_vma=False,
    )
```

```python
import functools

import jax
import jax.numpy as jnp
from jax import lax
from jax.experimental import pallas as pl
from jax.experimental.pallas import tpu as pltpu
from jax.sharding import PartitionSpec as P

GROUP = 128
EPSILON = 1e-06
F32 = jnp.float32
BF16 = jnp.bfloat16
MESH = pl.DeviceIdType.MESH


def dot(a, b, over):
    return lax.dot_general(a, b, (over, ((), ())), preferred_element_type=F32)


def nn(a, b):
    return dot(a, b, ((1,), (0,)))


def nt(a, b):
    return dot(a, b, ((1,), (1,)))


def tn(a, b):
    return dot(a, b, ((0,), (0,)))


def kernel(
    sizes,
    q_hbm, k_hbm, v_hbm, g_hbm, decay_hbm, gain_hbm,
    out, gq, gk, gv,
    q, k, v, g, decay, gain,
    mask, weights, dots, attn, grad, part, value_part, key_part,
    rise, tail, fresh, states, backs, wide_k, wide_q, plain_q,
    factor,
    pack, pair_in, joined, seen, made, came, pair_out, incoming,
    pack2, pair_in2, joined2, seen2, made2, came2, pair_out2, incoming2,
    sums, sums_x, sums2, sums_z,
    in_sem, send_sem, recv_sem,
):
    ranks, inner_size, outer_size, blocks, features = sizes
    rows = 2 * GROUP
    pos = lax.axis_index("ctx")
    head = lax.axis_index("head")
    outer, inner = head // inner_size, head % inner_size

    chips = ranks // 2
    chip, core = pos // 2, pos % 2
    partner = {"ctx": pos + 1 - 2 * core}
    order = sorted(range(1, chips), key=lambda s: -min(s, chips - s))
    chip_peers = {s: lax.rem(chip + s, chips) for s in order}
    ctx_peers = {s: {"ctx": chip_peers[s] * 2 + core} for s in order}
    x_peers = {s: outer * inner_size + lax.rem(inner + s, inner_size) for s in range(1, inner_size)}
    z_peers = {s: lax.rem(outer + s, outer_size) * inner_size + inner for s in range(1, outer_size)}

    loads = []
    pairs = (k_hbm, k), (v_hbm, v), (q_hbm, q), (g_hbm, g), (gain_hbm, gain), (decay_hbm, decay)
    for i, (src, dst) in reversed(list(enumerate(pairs))):
        loads.insert(0, pltpu.make_async_copy(src, dst, in_sem.at[i]))
        loads[0].start()

    barrier = pltpu.get_barrier_semaphore()
    for where in [ctx_peers[s] for s in order] + [partner]:
        pl.semaphore_signal(barrier, 1, device_id=where, device_id_type=MESH)
    for peer in list(x_peers.values()) + list(z_peers.values()):
        pl.semaphore_signal(barrier, 1, device_id={"head": peer}, device_id_type=MESH)

    def send(stage, s, src, dst, where):
        copy = pltpu.make_async_remote_copy(
            src_ref=src, dst_ref=dst,
            send_sem=send_sem.at[stage, s], recv_sem=recv_sem.at[stage, s],
            device_id=where, device_id_type=MESH,
        )
        copy.start()
        return copy

    row = lax.broadcasted_iota(jnp.int32, (rows, 128), 0)
    lane = lax.broadcasted_iota(jnp.int32, (rows, 128), 1)
    even = (row % 2) == 0
    token = row // 2
    big_row = lax.broadcasted_iota(jnp.int32, (rows, rows), 0)
    big_col = lax.broadcasted_iota(jnp.int32, (rows, rows), 1)

    def block(c):
        return pl.ds(c * rows, rows)

    def wide(x):
        return jnp.concatenate(
            [jnp.where(even, x, 0.0).astype(BF16), jnp.where(even, 0.0, x).astype(BF16)], axis=1
        )

    def own_head(x):
        return jnp.where(even, x[:, :128], x[:, 128:])

    loads[5].wait()
    block_decay = []
    total = jnp.zeros((2, 1), F32)
    cums = []
    for c in range(blocks):
        a = decay[:, c * GROUP:(c + 1) * GROUP]
        spread = jnp.where(even, a[0:1, :], a[1:2, :])
        cum = jnp.sum(jnp.where(lane <= token, spread, 0.0), axis=1, keepdims=True)
        end = jnp.sum(a, axis=1, keepdims=True)
        total = total + end
        end_rows = jnp.where(even, end[0:1, :], end[1:2, :])
        cum_full = jnp.broadcast_to(cum, (rows, 128))
        rise[c] = jnp.exp(cum_full)
        tail[c] = jnp.exp(end_rows - cum_full)
        block_decay.append(
            jnp.exp(jnp.where(row < 128, end[0:1, :], end[1:2, :]))
        )
        cums.append(cum)
    own_factor = jnp.exp(total)

    loads[0].wait()
    loads[1].wait()
    state = jnp.zeros((rows, 128), F32)
    for c in range(blocks):
        decayed = k[block(c), :].astype(F32) * tail[c]
        term = tn(wide(decayed), v[block(c), :])
        fresh[c] = term
        state = term if c == 0 else block_decay[c] * state + term
    per = 128 // chips
    pl.semaphore_wait(barrier, chips + (inner_size - 1) + (outer_size - 1))
    copies = []
    even_core = core == 0

    def arrive(sent):
        for copy in sent:
            copy.wait_recv()

    def exchange(stage, state, bufs, forward, covers):
        packed, paired, whole, held, prefix, back, passed, result = bufs
        packed[:, :128, :] = state.reshape(2, 128, 128)
        packed[0, 128:, :] = jnp.broadcast_to(own_factor[0:1, :], (8, 128))
        packed[1, 128:, :] = jnp.broadcast_to(own_factor[1:2, :], (8, 128))
        pair = send(7, stage, packed.at[1 - core], paired, partner)
        copies.append(pair)
        covers[0]()
        pair.wait_recv()
        mine, other = packed[core], paired[...]
        low = jnp.where(even_core, mine, other)
        high = jnp.where(even_core, other, mine)
        low_factor, high_factor = low[128:129, :], high[128:129, :]
        low, high = low[:128, :], high[:128, :]
        joint = high_factor * low + high if forward else low_factor * high + low
        whole[...] = joint.reshape(chips, per, 128)
        held[chip] = whole[chip]
        sent = [send(stage, s, whole.at[chip_peers[s]], held.at[chip], ctx_peers[s]) for s in order]
        if forward:
            factor[chip] = low_factor * high_factor
            sent += [send(0, s, factor.at[chip], factor.at[chip], ctx_peers[s]) for s in order]
        copies.extend(sent)
        covers[1]()
        arrive(sent)
        steps = list(range(chips)) if forward else list(reversed(range(chips)))
        carry = jnp.zeros((per, 128), F32)
        for n in steps:
            prefix[n] = carry
            if n != steps[-1]:
                carry = factor[n] * carry + held[n]
        back[chip] = prefix[chip]
        sent = [send(stage + 1, s, prefix.at[chip_peers[s]], back.at[chip], ctx_peers[s]) for s in order]
        copies.extend(sent)
        covers[2]()
        arrive(sent)
        first = back[...].reshape(128, 128)
        later = low_factor * first + low if forward else high_factor * first + high
        own_first = even_core if forward else core == 1
        passed[...] = jnp.where(own_first, later, first)
        pair = send(7, stage + 1, passed, result.at[core], partner)
        copies.append(pair)
        result[core] = jnp.where(own_first, first, later)
        pair.wait_recv()
        return result[...].reshape(rows, 128)

    same = (big_row % 2 == big_col % 2) & (big_row >= big_col)

    def local_forward(c):
        cum = jnp.broadcast_to(cums[c], (rows, rows))
        across = jnp.sum(jnp.where(big_row == big_col, cum, 0.0), axis=0, keepdims=True)
        m = jnp.where(same, jnp.exp(jnp.where(same, cum - across, 0.0)), 0.0)
        mask[c] = m
        w = (nt(q[block(c), :], k[block(c), :]) * m).astype(BF16)
        weights[c] = w
        part[c] = nn(w, v[block(c), :])

    def cover_first():
        loads[2].wait()
        local_forward(0)

    def cover_second():
        for c in range(1, blocks):
            local_forward(c)

    def cover_third():
        for c in range(blocks):
            q_block = q[block(c), :].astype(F32)
            wide_k[c] = wide(k[block(c), :].astype(F32))
            wide_q[c] = wide(q_block * rise[c])
            plain_q[c] = wide(q_block)
        loads[3].wait()
        loads[4].wait()

    state = exchange(
        3, state, (pack, pair_in, joined, seen, made, came, pair_out, incoming), True,
        (cover_first, cover_second, cover_third),
    )
    for c in range(blocks):
        if c:
            state = block_decay[c - 1] * state + fresh[c - 1]
        states[c] = state.astype(BF16)

    gain_rows = jnp.where(even, gain[0:1, :], gain[1:2, :])
    pick = token == lane

    def per_token(x):
        col = jnp.sum(x, axis=1, keepdims=True)
        return jnp.sum(jnp.where(pick, col, 0.0), axis=0, keepdims=True)

    for c in range(blocks):
        carried = nn(plain_q[c], states[c])
        a_bf = (part[c] + carried * rise[c]).astype(BF16)
        attn[c] = a_bf
        a = a_bf.astype(F32)
        ga = gain_rows * a
        sums[3 * c:3 * c + 1, :] = per_token(a * a)
        sums[3 * c + 1:3 * c + 2, :] = per_token(ga * g[block(c), :].astype(F32))
        sums[3 * c + 2:3 * c + 3, :] = per_token(ga * ga)

    x_sent = [send(1, s, sums, sums_x.at[s - 1], {"head": x_peers[s]}) for s in x_peers]
    copies += x_sent
    arrive(x_sent)
    acc = sums[...]
    for s in x_peers:
        acc = acc + sums_x[s - 1]
    sums2[...] = acc
    z_sent = [send(2, s, sums2, sums_z.at[s - 1], {"head": z_peers[s]}) for s in z_peers]
    copies += z_sent
    arrive(z_sent)
    for s in z_peers:
        acc = acc + sums_z[s - 1]

    def to_rows(x):
        return jnp.sum(jnp.where(pick, x, 0.0), axis=1, keepdims=True)

    for c in range(blocks):
        inv = lax.rsqrt(acc[3 * c:3 * c + 1, :] / features + EPSILON)
        total_inner = acc[3 * c + 1:3 * c + 2, :] + inv * acc[3 * c + 2:3 * c + 3, :]
        shrink = inv * inv * inv * total_inner / features
        inv_col = to_rows(inv)
        shrink_col = to_rows(shrink)
        a = attn[c].astype(F32)
        o = (a * inv_col * gain_rows).astype(BF16)
        out[block(c), :] = o
        scaled = gain_rows * (g[block(c), :].astype(F32) + o.astype(F32))
        grad[c] = (inv_col * scaled - a * shrink_col).astype(BF16)

    for c in reversed(range(blocks)):
        term = tn(wide_q[c], grad[c])
        fresh[c] = term
        state = term if c == blocks - 1 else block_decay[c] * state + term
    def local_dots(c):
        d = (nt(grad[c], v[block(c), :]) * mask[c]).astype(BF16)
        dots[c] = d
        carried = own_head(nt(grad[c], states[c]))
        gq[block(c), :] = (nn(d, k[block(c), :]) + carried * rise[c]).astype(BF16)

    def local_backward(c):
        key_part[c] = tn(dots[c], q[block(c), :])
        value_part[c] = tn(weights[c], grad[c])

    def back_second():
        for c in range(1, blocks):
            local_dots(c)
        local_backward(0)

    def back_third():
        for c in range(1, blocks):
            local_backward(c)

    state = exchange(
        5, state, (pack2, pair_in2, joined2, seen2, made2, came2, pair_out2, incoming2), False,
        (lambda: local_dots(0), back_second, back_third),
    )
    for c in reversed(range(blocks)):
        if c < blocks - 1:
            state = block_decay[c + 1] * state + fresh[c + 1]
        backs[c] = state.astype(BF16)
    for c in range(blocks):
        key_carried = own_head(nt(v[block(c), :], backs[c]))
        gk[block(c), :] = (key_part[c] + key_carried * tail[c]).astype(BF16)
        value_carried = nn(wide_k[c], backs[c])
        gv[block(c), :] = (value_part[c] + value_carried * tail[c]).astype(BF16)
    for copy in copies:
        copy.wait_send()


def write_out(a, b, c, d, oa, ob, oc, od, sem):
    copies = [
        pltpu.make_async_copy(src, dst, sem.at[i])
        for i, (src, dst) in enumerate(((a, oa), (b, ob), (c, oc), (d, od)))
    ]
    for copy in copies:
        copy.start()
    for copy in copies:
        copy.wait()


def per_device(ranks, head_ranks, inner_size, query_rows, key_matrix, value_rows, decay_log, norm_gain, grad_out):
    tokens, heads, size = query_rows.shape
    blocks = tokens // GROUP
    rows = 2 * GROUP
    chips = ranks // 2
    outer_size = head_ranks // inner_size
    flat = (tokens * heads, size)
    sizes = (ranks, inner_size, outer_size, blocks, heads * head_ranks * size)
    vm = pltpu.VMEM
    sum_rows = 3 * blocks
    any_spec = pl.BlockSpec(memory_space=pl.ANY)
    vmem_spec = pl.BlockSpec(memory_space=pltpu.VMEM)
    state_slots = [vm((2, 136, 128), F32), vm((136, 128), F32)]
    state_slots += [vm((chips, 128 // chips, 128), F32)] * 4
    state_slots += [vm((128, 128), F32), vm((2, 128, 128), F32)]
    results = pl.pallas_call(
        functools.partial(kernel, sizes),
        out_shape=[pltpu.VMEM(flat, BF16)] * 4,
        in_specs=[any_spec] * 6,
        out_specs=[vmem_spec] * 4,
        scratch_shapes=[vm(flat, BF16)] * 4
        + [
            vm(decay_log.T.shape, F32),
            vm(norm_gain.shape, F32),
            vm((blocks, rows, rows), F32),
            vm((blocks, rows, rows), BF16),
            vm((blocks, rows, rows), BF16),
            vm((blocks, rows, 128), BF16),
            vm((blocks, rows, 128), BF16),
            vm((blocks, rows, 128), F32),
            vm((blocks, rows, 128), F32),
            vm((blocks, rows, 128), F32),
            vm((blocks, rows, 128), F32),
            vm((blocks, rows, 128), F32),
            vm((blocks, rows, 128), F32),
            vm((blocks, rows, 128), BF16),
            vm((blocks, rows, 128), BF16),
            vm((blocks, rows, rows), BF16),
            vm((blocks, rows, rows), BF16),
            vm((blocks, rows, rows), BF16),
            vm((chips, 1, 128), F32),
        ]
        + state_slots
        + state_slots
        + [
            vm((sum_rows, 128), F32),
            vm((inner_size - 1, sum_rows, 128), F32),
            vm((sum_rows, 128), F32),
            vm((outer_size - 1, sum_rows, 128), F32),
            pltpu.SemaphoreType.DMA((6,)),
            pltpu.SemaphoreType.DMA((8, 8)),
            pltpu.SemaphoreType.DMA((8, 8)),
        ],
        compiler_params=pltpu.CompilerParams(collective_id=0, has_side_effects=True),
        name="lightning",
    )(
        query_rows.reshape(flat),
        key_matrix.reshape(flat),
        value_rows.reshape(flat),
        grad_out.reshape(flat),
        decay_log.T,
        norm_gain,
    )
    results = pl.pallas_call(
        write_out,
        out_shape=[jax.ShapeDtypeStruct(flat, BF16)] * 4,
        in_specs=[vmem_spec] * 4,
        out_specs=[any_spec] * 4,
        scratch_shapes=[pltpu.SemaphoreType.DMA((4,))],
        name="write_out",
    )(*[pltpu.with_memory_space_constraint(r, pltpu.VMEM) for r in results])
    return tuple(r.reshape(tokens, heads, size) for r in results)


def solution(mesh):
    ranks, head_ranks = mesh.shape["ctx"], mesh.shape["head"]
    inner_size = 4 if head_ranks % 4 == 0 and head_ranks > 4 else 1
    rows = P("ctx", "head", None)
    return jax.shard_map(
        functools.partial(per_device, ranks, head_ranks, inner_size),
        mesh=mesh,
        in_specs=(rows, rows, rows, P("ctx", "head"), P("head", None), rows),
        out_specs=(rows,) * 4,
        check_vma=False,
    )
```

```python
import functools

import jax
import jax.numpy as jnp
from jax import lax
from jax.experimental import pallas as pl
from jax.experimental.pallas import tpu as pltpu
from jax.sharding import PartitionSpec as P

GROUP = 128
EPSILON = 1e-06
F32 = jnp.float32
BF16 = jnp.bfloat16
MESH = pl.DeviceIdType.MESH


def dot(a, b, over):
    return lax.dot_general(a, b, (over, ((), ())), preferred_element_type=F32)


def nn(a, b):
    return dot(a, b, ((1,), (0,)))


def nt(a, b):
    return dot(a, b, ((1,), (1,)))


def tn(a, b):
    return dot(a, b, ((0,), (0,)))


def kernel(
    sizes,
    q_hbm, k_hbm, v_hbm, g_hbm, decay_hbm, gain_hbm,
    out, gq, gk, gv,
    q, k, v, g, decay, gain,
    mask, weights, dots, attn, grad, part, value_part, key_part,
    rise, tail, fresh, states, backs, wide_k, wide_q, plain_q,
    factor,
    pack, pair_in, joined, seen, made, came, pair_out, incoming,
    pack2, pair_in2, joined2, seen2, made2, came2, pair_out2, incoming2,
    sums, sums_x, sums2, sums_z,
    in_sem, send_sem, recv_sem,
):
    ranks, inner_size, outer_size, blocks, features = sizes
    rows = 2 * GROUP
    pos = lax.axis_index("ctx")
    head = lax.axis_index("head")
    outer, inner = head // inner_size, head % inner_size

    chips = ranks // 2
    chip, core = pos // 2, pos % 2
    partner = {"ctx": pos + 1 - 2 * core}
    far_first = lambda n: sorted(range(1, n), key=lambda s: -min(s, n - s))
    order = far_first(chips)
    chip_peers = {s: lax.rem(chip + s, chips) for s in order}
    ctx_peers = {s: {"ctx": chip_peers[s] * 2 + core} for s in order}
    x_peers = {s: outer * inner_size + lax.rem(inner + s, inner_size) for s in far_first(inner_size)}
    z_peers = {s: lax.rem(outer + s, outer_size) * inner_size + inner for s in far_first(outer_size)}

    loads = {}
    pairs = (k_hbm, k), (v_hbm, v), (q_hbm, q), (g_hbm, g), (gain_hbm, gain), (decay_hbm, decay)
    for i in (5, 0, 1, 2, 3, 4):
        src, dst = pairs[i]
        loads[i] = pltpu.make_async_copy(src, dst, in_sem.at[i])
        loads[i].start()

    barrier = pltpu.get_barrier_semaphore()
    greet = [ctx_peers[s] for s in order]
    greet += [{"head": peer} for peer in list(z_peers.values()) + list(x_peers.values())]
    for where in greet + [partner]:
        pl.semaphore_signal(barrier, 1, device_id=where, device_id_type=MESH)

    slots = iter(range(send_sem.shape[0]))

    def send(src, dst, where):
        slot = next(slots)
        copy = pltpu.make_async_remote_copy(
            src_ref=src, dst_ref=dst,
            send_sem=send_sem.at[slot], recv_sem=recv_sem.at[slot],
            device_id=where, device_id_type=MESH,
        )
        copy.start()
        return copy

    row = lax.broadcasted_iota(jnp.int32, (rows, 128), 0)
    lane = lax.broadcasted_iota(jnp.int32, (rows, 128), 1)
    even = (row % 2) == 0
    token = row // 2
    big_row = lax.broadcasted_iota(jnp.int32, (rows, rows), 0)
    big_col = lax.broadcasted_iota(jnp.int32, (rows, rows), 1)

    def block(c):
        return pl.ds(c * rows, rows)

    def wide(x):
        return jnp.concatenate(
            [jnp.where(even, x, 0.0).astype(BF16), jnp.where(even, 0.0, x).astype(BF16)], axis=1
        )

    def own_head(x):
        return jnp.where(even, x[:, :128], x[:, 128:])

    loads[5].wait()
    block_decay = []
    total = jnp.zeros((2, 1), F32)
    cums = []
    for c in range(blocks):
        a = decay[:, c * GROUP:(c + 1) * GROUP]
        spread = jnp.where(even, a[0:1, :], a[1:2, :])
        cum = jnp.sum(jnp.where(lane <= token, spread, 0.0), axis=1, keepdims=True)
        end = jnp.sum(a, axis=1, keepdims=True)
        total = total + end
        end_rows = jnp.where(even, end[0:1, :], end[1:2, :])
        cum_full = jnp.broadcast_to(cum, (rows, 128))
        tail[c] = jnp.exp(end_rows - cum_full)
        block_decay.append(
            jnp.exp(jnp.where(row < 128, end[0:1, :], end[1:2, :]))
        )
        cums.append(cum)
    own_factor = jnp.exp(total)

    loads[0].wait()
    loads[1].wait()
    state = jnp.zeros((rows, 128), F32)
    for c in range(blocks):
        decayed = k[block(c), :].astype(F32) * tail[c]
        term = tn(wide(decayed), v[block(c), :])
        fresh[c] = term
        state = term if c == 0 else block_decay[c] * state + term
    per = 128 // chips
    pl.semaphore_wait(barrier, chips + (inner_size - 1) + (outer_size - 1))
    copies = []
    even_core = core == 0

    def arrive(sent):
        for copy in sent:
            copy.wait_recv()

    def exchange(state, bufs, forward, covers):
        packed, paired, whole, held, prefix, back, passed, result = bufs
        packed[:, :128, :] = state.reshape(2, 128, 128)
        packed[0, 128:, :] = jnp.broadcast_to(own_factor[0:1, :], (8, 128))
        packed[1, 128:, :] = jnp.broadcast_to(own_factor[1:2, :], (8, 128))
        pair = send(packed.at[1 - core], paired, partner)
        copies.append(pair)
        covers[0]()
        pair.wait_recv()
        mine, other = packed[core], paired[...]
        low = jnp.where(even_core, mine, other)
        high = jnp.where(even_core, other, mine)
        low_factor, high_factor = low[128:129, :], high[128:129, :]
        low, high = low[:128, :], high[:128, :]
        joint = high_factor * low + high if forward else low_factor * high + low
        whole[...] = joint.reshape(chips, per, 128)
        held[chip] = whole[chip]
        sent = [send(whole.at[chip_peers[s]], held.at[chip], ctx_peers[s]) for s in order]
        if forward:
            factor[chip] = low_factor * high_factor
            sent += [send(factor.at[chip], factor.at[chip], ctx_peers[s]) for s in order]
        copies.extend(sent)
        covers[1]()
        arrive(sent)
        steps = list(range(chips)) if forward else list(reversed(range(chips)))
        carry = jnp.zeros((per, 128), F32)
        for n in steps:
            prefix[n] = carry
            if n != steps[-1]:
                carry = factor[n] * carry + held[n]
        back[chip] = prefix[chip]
        sent = [send(prefix.at[chip_peers[s]], back.at[chip], ctx_peers[s]) for s in order]
        copies.extend(sent)
        covers[2]()
        arrive(sent)
        first = back[...].reshape(128, 128)
        later = low_factor * first + low if forward else high_factor * first + high
        own_first = even_core if forward else core == 1
        passed[...] = jnp.where(own_first, later, first)
        pair = send(passed, result.at[core], partner)
        copies.append(pair)
        result[core] = jnp.where(own_first, first, later)
        pair.wait_recv()
        return result[...].reshape(rows, 128)

    same = (big_row % 2 == big_col % 2) & (big_row >= big_col)

    def local_forward(c):
        rise[c] = jnp.exp(jnp.broadcast_to(cums[c], (rows, 128)))
        cum = jnp.broadcast_to(cums[c], (rows, rows))
        across = jnp.sum(jnp.where(big_row == big_col, cum, 0.0), axis=0, keepdims=True)
        m = jnp.where(same, jnp.exp(jnp.where(same, cum - across, 0.0)), 0.0)
        mask[c] = m
        w = (nt(q[block(c), :], k[block(c), :]) * m).astype(BF16)
        weights[c] = w
        part[c] = nn(w, v[block(c), :])

    def cover_first():
        loads[2].wait()
        local_forward(0)

    def cover_second():
        for c in range(1, blocks):
            local_forward(c)

    def cover_third():
        for c in range(blocks):
            q_block = q[block(c), :].astype(F32)
            wide_k[c] = wide(k[block(c), :].astype(F32))
            wide_q[c] = wide(q_block * rise[c])
            plain_q[c] = wide(q_block)
        loads[3].wait()
        loads[4].wait()

    state = exchange(
        state, (pack, pair_in, joined, seen, made, came, pair_out, incoming), True,
        (cover_first, cover_second, cover_third),
    )
    for c in range(blocks):
        if c:
            state = block_decay[c - 1] * state + fresh[c - 1]
        states[c] = state.astype(BF16)

    gain_rows = jnp.where(even, gain[0:1, :], gain[1:2, :])
    pick = token == lane

    def per_token(x):
        col = jnp.sum(x, axis=1, keepdims=True)
        return jnp.sum(jnp.where(pick, col, 0.0), axis=0, keepdims=True)

    for c in range(blocks):
        carried = nn(plain_q[c], states[c])
        a_bf = (part[c] + carried * rise[c]).astype(BF16)
        attn[c] = a_bf
        a = a_bf.astype(F32)
        ga = gain_rows * a
        sums[3 * c:3 * c + 1, :] = per_token(a * a)
        sums[3 * c + 1:3 * c + 2, :] = per_token(ga * g[block(c), :].astype(F32))
        sums[3 * c + 2:3 * c + 3, :] = per_token(ga * ga)

    x_sent = [send(sums, sums_x.at[s - 1], {"head": x_peers[s]}) for s in x_peers]
    copies += x_sent
    arrive(x_sent)
    acc = sums[...]
    for s in x_peers:
        acc = acc + sums_x[s - 1]
    sums2[...] = acc
    z_sent = [send(sums2, sums_z.at[s - 1], {"head": z_peers[s]}) for s in z_peers]
    copies += z_sent
    arrive(z_sent)
    for s in z_peers:
        acc = acc + sums_z[s - 1]

    def to_rows(x):
        return jnp.sum(jnp.where(pick, x, 0.0), axis=1, keepdims=True)

    for c in range(blocks):
        inv = lax.rsqrt(acc[3 * c:3 * c + 1, :] / features + EPSILON)
        total_inner = acc[3 * c + 1:3 * c + 2, :] + inv * acc[3 * c + 2:3 * c + 3, :]
        shrink = inv * inv * inv * total_inner / features
        inv_col = to_rows(inv)
        shrink_col = to_rows(shrink)
        a = attn[c].astype(F32)
        o = (a * inv_col * gain_rows).astype(BF16)
        out[block(c), :] = o
        scaled = gain_rows * (g[block(c), :].astype(F32) + o.astype(F32))
        grad[c] = (inv_col * scaled - a * shrink_col).astype(BF16)

    for c in reversed(range(blocks)):
        term = tn(wide_q[c], grad[c])
        fresh[c] = term
        state = term if c == blocks - 1 else block_decay[c] * state + term
    def local_dots(c):
        d = (nt(grad[c], v[block(c), :]) * mask[c]).astype(BF16)
        dots[c] = d
        carried = own_head(nt(grad[c], states[c]))
        gq[block(c), :] = (nn(d, k[block(c), :]) + carried * rise[c]).astype(BF16)

    def local_backward(c):
        key_part[c] = tn(dots[c], q[block(c), :])
        value_part[c] = tn(weights[c], grad[c])

    def back_second():
        for c in range(1, blocks):
            local_dots(c)
        local_backward(0)

    def back_third():
        for c in range(1, blocks):
            local_backward(c)

    state = exchange(
        state, (pack2, pair_in2, joined2, seen2, made2, came2, pair_out2, incoming2), False,
        (lambda: local_dots(0), back_second, back_third),
    )
    for c in reversed(range(blocks)):
        if c < blocks - 1:
            state = block_decay[c + 1] * state + fresh[c + 1]
        backs[c] = state.astype(BF16)
    for c in range(blocks):
        key_carried = own_head(nt(v[block(c), :], backs[c]))
        gk[block(c), :] = (key_part[c] + key_carried * tail[c]).astype(BF16)
        value_carried = nn(wide_k[c], backs[c])
        gv[block(c), :] = (value_part[c] + value_carried * tail[c]).astype(BF16)
    for copy in copies:
        copy.wait_send()


def write_out(a, b, c, d, oa, ob, oc, od, sem):
    copies = [
        pltpu.make_async_copy(src, dst, sem.at[i])
        for i, (src, dst) in enumerate(((a, oa), (b, ob), (c, oc), (d, od)))
    ]
    for copy in copies:
        copy.start()
    for copy in copies:
        copy.wait()


def per_device(ranks, head_ranks, inner_size, query_rows, key_matrix, value_rows, decay_log, norm_gain, grad_out):
    tokens, heads, size = query_rows.shape
    blocks = tokens // GROUP
    rows = 2 * GROUP
    chips = ranks // 2
    outer_size = head_ranks // inner_size
    flat = (tokens * heads, size)
    sizes = (ranks, inner_size, outer_size, blocks, heads * head_ranks * size)
    vm = pltpu.VMEM
    sum_rows = 3 * blocks
    slots = 4 + 5 * (chips - 1) + inner_size + outer_size - 2
    any_spec = pl.BlockSpec(memory_space=pl.ANY)
    vmem_spec = pl.BlockSpec(memory_space=pltpu.VMEM)
    state_slots = [vm((2, 136, 128), F32), vm((136, 128), F32)]
    state_slots += [vm((chips, 128 // chips, 128), F32)] * 4
    state_slots += [vm((128, 128), F32), vm((2, 128, 128), F32)]
    results = pl.pallas_call(
        functools.partial(kernel, sizes),
        out_shape=[pltpu.VMEM(flat, BF16)] * 4,
        in_specs=[any_spec] * 6,
        out_specs=[vmem_spec] * 4,
        scratch_shapes=[vm(flat, BF16)] * 4
        + [
            vm(decay_log.T.shape, F32),
            vm(norm_gain.shape, F32),
            vm((blocks, rows, rows), F32),
            vm((blocks, rows, rows), BF16),
            vm((blocks, rows, rows), BF16),
            vm((blocks, rows, 128), BF16),
            vm((blocks, rows, 128), BF16),
            vm((blocks, rows, 128), F32),
            vm((blocks, rows, 128), F32),
            vm((blocks, rows, 128), F32),
            vm((blocks, rows, 128), F32),
            vm((blocks, rows, 128), F32),
            vm((blocks, rows, 128), F32),
            vm((blocks, rows, 128), BF16),
            vm((blocks, rows, 128), BF16),
            vm((blocks, rows, rows), BF16),
            vm((blocks, rows, rows), BF16),
            vm((blocks, rows, rows), BF16),
            vm((chips, 1, 128), F32),
        ]
        + state_slots
        + state_slots
        + [
            vm((sum_rows, 128), F32),
            vm((inner_size - 1, sum_rows, 128), F32),
            vm((sum_rows, 128), F32),
            vm((outer_size - 1, sum_rows, 128), F32),
            pltpu.SemaphoreType.DMA((6,)),
            pltpu.SemaphoreType.DMA((slots,)),
            pltpu.SemaphoreType.DMA((slots,)),
        ],
        compiler_params=pltpu.CompilerParams(collective_id=0, has_side_effects=True),
        name="lightning",
    )(
        query_rows.reshape(flat),
        key_matrix.reshape(flat),
        value_rows.reshape(flat),
        grad_out.reshape(flat),
        decay_log.T,
        norm_gain,
    )
    results = pl.pallas_call(
        write_out,
        out_shape=[jax.ShapeDtypeStruct(flat, BF16)] * 4,
        in_specs=[vmem_spec] * 4,
        out_specs=[any_spec] * 4,
        scratch_shapes=[pltpu.SemaphoreType.DMA((4,))],
        name="write_out",
    )(*[pltpu.with_memory_space_constraint(r, pltpu.VMEM) for r in results])
    return tuple(r.reshape(tokens, heads, size) for r in results)


def solution(mesh):
    ranks, head_ranks = mesh.shape["ctx"], mesh.shape["head"]
    inner_size = 4 if head_ranks % 4 == 0 and head_ranks > 4 else 1
    rows = P("ctx", "head", None)
    return jax.shard_map(
        functools.partial(per_device, ranks, head_ranks, inner_size),
        mesh=mesh,
        in_specs=(rows, rows, rows, P("ctx", "head"), P("head", None), rows),
        out_specs=(rows,) * 4,
        check_vma=False,
    )
```
